32 devices in a mesh: row: 4 (over y, x), col: 8 (over z, core).
Axes of the slice: x: 2, y: 2, z: 4, core: 2. Of those that a mesh axis runs over, the one named last changes fastest.
Arguments:
- band_factors: bfloat16 [48, 48, 8, 256], P('col'), may hold values from -6 to 6
- pair_density: bfloat16 [48, 48, 16, 256], P('col'), may hold values from -6 to 6
- screened: bfloat16 [48, 48, 256, 256], P('col'), may hold values from -1 to 3, as said below
- coulomb: float32 [256], replicated, may hold values from 0.2 to 2
- window_mask: int32 [6, 48, 48], P(None, 'row'), may hold values 0 or 1
- trial_vector: bfloat16 [16, 48, 48], P(None, 'col'), may hold values from -0.0013809204 to 0.0013809204
Outputs:
- row_image: float32 [16, 6, 48], P('col', None, 'row')
- col_image: float32 [16, 48, 48], P(None, 'col', 'row')
The draws below stay inside these ranges and needn't reach their ends.
Inputs may be any that keep to these rules, and one draw needn't show every extreme that they name: `screened`: every block is symmetric.
All inputs are finite; a program needn't handle non-finite values. No bound on the sum of `window_mask` on one device may be relied on, other than what follows from the above.
Results may differ from the reference program's by a relative error of at most 0.0041.
Values may be sent and summed in bfloat16 or wider, within the bound.
No kernel may reach another device: no remote copies, remote signals or barrier semaphores. Data moves between devices by JAX's collectives and lax.ppermute only.
A program may use at most 512 MiB of HBM per device.

```python
import math
import jax
import jax.numpy as jnp
from jax import lax

G = 256
BANDS = 8
PAIRS = 16
MESH = 48
CR = 6
NK = 2304
N_COL = 8


def draw_screened(key, part):
    first_key, second_key = jax.random.split(jax.random.fold_in(key, 11))
    base = jax.random.normal(first_key, (MESH, MESH, G, G), jnp.float32)
    symmetric = (base + jnp.swapaxes(base, 2, 3)) * (0.5 / math.sqrt(G))
    diagonal = jnp.exp(jax.random.uniform(second_key, (MESH, MESH, G), jnp.float32, -0.7, 0.7))
    return (symmetric + diagonal[..., None] * jnp.eye(G, dtype=jnp.float32)).astype(jnp.bfloat16)


def plant(drawn, rng, smallest, top_value):
    longest = drawn.shape.index(max(drawn.shape))
    spots = []
    for shift in (0, 1):
        where = [jax.random.randint(jax.random.fold_in(rng, axis), (), 0, length) for axis, length in enumerate(drawn.shape)]
        where[longest] = (where[longest] + shift) % drawn.shape[longest]
        spots.append(tuple(where))
    return drawn.at[spots[0]].set(smallest).at[spots[1]].set(top_value)


def block_levels(own_key, dims, cuts, smallest, high):
    def one(position, parts):
        heights = jax.random.uniform(jax.random.fold_in(jax.random.fold_in(own_key, 6), position), (parts,), jnp.float32, smallest / len(cuts), high / len(cuts))
        return jnp.repeat(jnp.exp(heights), dims[position] // parts).reshape((-1,) + (1,) * (len(dims) - position - 1))

    level = one(*cuts[0])
    for cut in cuts[1:]:
        level = level * one(*cut)
    return level


def scatter_about(stream_key, extent, width, most, cuts=(), kind=jnp.bfloat16):
    result = width * jax.random.normal(stream_key, extent, jnp.float32)
    if cuts:
        result = result * block_levels(stream_key, extent, cuts, -0.22, 0.18)
    return jnp.clip(result, -most, most).astype(kind)


def setup_inputs(seed: int = 0) -> dict:
    streams_of = jax.random.split(jax.random.key(seed), 7)
    return {
        "band_factors": scatter_about(streams_of[0], (MESH, MESH, BANDS, G), 1.0, 6.0, ((0, 8),)),
        "pair_density": scatter_about(streams_of[1], (MESH, MESH, PAIRS, G), 1.0, 6.0, ((0, 8),)),
        "screened": draw_screened(jax.random.fold_in(streams_of[6], 71), 0),
        "coulomb": jnp.clip(jnp.exp(jax.random.uniform(streams_of[3], (G,), jnp.float32, math.log(0.2), math.log(2.0))), 0.2, 2.0),
        "window_mask": plant((jax.random.randint(streams_of[4], (CR, MESH, MESH), 0, 4) < 3).astype(jnp.int32), jax.random.fold_in(streams_of[4], 1), 0, 1),
        "trial_vector": scatter_about(streams_of[5], (PAIRS, MESH, MESH), ((2 * NK * PAIRS * G) ** -0.5), 0.0013809204, ((1, 8),)),
    }


HIGHEST_PRECISION = lax.Precision.HIGHEST


def pair_block(row_bands, row_pairs, row_trial, row_line, col_bands, col_pairs, col_trial, col_line, w_row, coulomb, mask_line):
    mesh_side = row_bands.shape[0]
    band_half = row_bands.shape[1] // 2
    fourier = row_bands.shape[2]
    offsets = jnp.arange(mesh_side, dtype=jnp.int32)
    places = (offsets[None, :] + offsets[:, None]) % mesh_side
    chosen_bands = jnp.take(col_bands, places, axis=0).astype(jnp.float32)
    chosen_pairs = jnp.take(col_pairs, places, axis=0).astype(jnp.float32)
    own_bands = row_bands.astype(jnp.float32)
    left_pair = (own_bands[None, :, :band_half, None, :] * chosen_bands[:, :, None, :band_half, :]).astype(jnp.bfloat16)
    right_pair = (own_bands[None, :, band_half:, None, :] * chosen_bands[:, :, None, band_half:, :]).astype(jnp.bfloat16)
    mixed_pair = jnp.einsum("qng,qgh->qnh", left_pair.reshape(mesh_side, -1, fourier).astype(jnp.float32), w_row.astype(jnp.float32)).astype(jnp.bfloat16)
    mixed_pair = mixed_pair.reshape(mesh_side, mesh_side, band_half, band_half, fourier)
    direct = jnp.einsum("qbach,qbvwh->qbvawc", mixed_pair.astype(jnp.float32), right_pair.astype(jnp.float32))
    direct = direct.reshape(mesh_side, mesh_side, band_half * band_half, band_half * band_half)
    scaled = (row_pairs.astype(jnp.float32) * coulomb).astype(jnp.bfloat16)
    exchange_term = jnp.einsum("bsg,qbug->qbsu", scaled.astype(jnp.float32), chosen_pairs)
    kernel = 2.0 * exchange_term - direct
    row_place = row_line * mesh_side + offsets
    col_place = col_line * mesh_side + places
    kept = (col_place >= row_place[None, :]) & (mask_line[None, :] > 0)
    kernel = jnp.where(kept[..., None, None], kernel, jnp.float32(0.0))
    col_values = jnp.take(col_trial.astype(jnp.float32), places, axis=1)
    row_part = jnp.einsum("qbsu,uqb->sb", kernel, col_values, precision=HIGHEST_PRECISION)
    strict = col_place > row_place[None, :]
    col_each = jnp.einsum("qbsu,sb->uqb", jnp.where(strict[..., None, None], kernel, jnp.float32(0.0)), row_trial.astype(jnp.float32), precision=HIGHEST_PRECISION)
    onehot = (places[:, :, None] == offsets[None, None, :]).astype(jnp.float32)
    col_part = jnp.einsum("uqb,qbc->uc", col_each, onehot, precision=HIGHEST_PRECISION)
    return row_part, col_part


def reference(band_factors, pair_density, screened, coulomb, window_mask, trial_vector):
    mesh_side = MESH
    first_line = MESH // 2
    band_lines = MESH // N_COL
    upper_lines = mesh_side - first_line
    row_lines = jnp.repeat(jnp.arange(band_lines, dtype=jnp.int32), upper_lines)
    col_lines = jnp.tile(first_line + jnp.arange(upper_lines, dtype=jnp.int32), band_lines)

    def per_pair(indices):
        panel_line, col_line = indices
        row_line = first_line + panel_line
        shift_line = (col_line - row_line) % mesh_side
        return pair_block(band_factors[row_line], pair_density[row_line], trial_vector[:, row_line], row_line, band_factors[col_line], pair_density[col_line], trial_vector[:, col_line], col_line, screened[shift_line], coulomb, window_mask[panel_line, :, col_line])

    row_parts, col_parts = lax.map(per_pair, (row_lines, col_lines))
    row_image = row_parts.reshape(band_lines, upper_lines, PAIRS, mesh_side).sum(axis=1).transpose(1, 0, 2)
    col_upper = col_parts.reshape(band_lines, upper_lines, PAIRS, mesh_side).sum(axis=0).transpose(1, 0, 2)
    col_image = jnp.concatenate([jnp.zeros((PAIRS, first_line, mesh_side), jnp.float32), col_upper], axis=1)
    return row_image, col_image
```

```python
import functools

import jax
import jax.numpy as jnp
from jax import lax
from jax.experimental import pallas as pl
from jax.experimental.pallas import tpu as pltpu
from jax.sharding import PartitionSpec as P

EXPLICIT = True
HIGHEST = lax.Precision.HIGHEST
F32 = jnp.float32
BF16 = jnp.bfloat16


def shape_plan(lines, row_width):
    best = None
    for copies in range(1, row_width + 1):
        if row_width % copies:
            continue
        used = copies * lines
        groups = -(-used // 8)
        waste = groups * 8 * (row_width // copies)
        if best is None or waste < best[0]:
            best = (waste, copies, groups)
    _, copies, groups = best
    return row_width // copies, copies, groups


def pair_kernel(plan, scal, w, mask, au, az, bu, bz, aw, bw, rout, cout, ra, cb):
    lines, stride, groups, side, batch, slots, depth = plan
    gap = pl.program_id(0)
    part = pl.program_id(1)
    offset = scal[0]
    active = scal[1]
    own = scal[2]
    half = au.shape[1]
    last = (gap == pl.num_programs(0) - 1) & (part == pl.num_programs(1) - 1)

    def multiply(chunks, loads, accs):
        if not EXPLICIT:
            for unit, make in chunks:
                yield jnp.dot(make(), loads[unit][1], preferred_element_type=F32)
            return
        started = [0, 0]
        pending = []

        def issue(unit, make):
            slot = accs[unit * slots + started[unit] % slots]
            stage = loads[unit][0] if started[unit] == 0 else None
            pltpu.matmul_acc_lhs(slot, make(), load_staged_rhs=stage)
            started[unit] += 1
            pending.append(slot)

        for unit, make in chunks[:depth]:
            issue(unit, make)
        for n in range(len(chunks)):
            if n + depth < len(chunks):
                issue(*chunks[n + depth])
            yield pltpu.matmul_pop(pending.pop(0))

    def sweep(units, gap_index, with_row, sign):
        chunks = []
        where = []
        for j in range(stride):
            for g in range(groups):
                for c in range(half):
                    for unit, _, q, base, _ in units:

                        def make(j=j, g=g, c=c, q=q, base=base):
                            mk = mask[0, q, j, g]
                            row = au[base + j, c, g] * jnp.concatenate([mk, mk], axis=1)
                            return jnp.concatenate([row] * (half // 2), axis=0) * bu[gap_index, j, g]

                        chunks.append((unit, make))
                        where.append((j, g, c, base))
        loads = {unit: (staged, weight) for unit, staged, _, _, weight in units}
        if not EXPLICIT:
            consume(multiply(chunks, loads, ()), where, gap_index, with_row, sign)
            return
        spaces = [pltpu.ACC(unit)((8 * half, au.shape[-1]), F32) for unit in (0, 1) for _ in range(slots)]
        pl.run_scoped(
            lambda *accs: consume(multiply(chunks, loads, accs), where, gap_index, with_row, sign), *spaces
        )

    def consume(products, where, gap_index, with_row, sign):
        total = None
        for n, m in enumerate(products):
            j, g, c, base = where[n]
            if with_row:
                p = m * bz[gap_index, j, g]
                s = p[0:8]
                for v in range(1, half):
                    s = s + p[8 * v : 8 * v + 8]
                ra[base + j, c, g] = ra[base + j, c, g] + s
            t = m * jnp.concatenate([az[base + j, c, g]] * half, axis=0)
            total = t if total is None else total + t
            if n + 1 == len(where) or where[n + 1][:2] != (j, g):
                if sign > 0:
                    cb[gap_index, j, g] = cb[gap_index, j, g] + total
                else:
                    cb[gap_index, j, g] = cb[gap_index, j, g] - total
                total = None

    def base_of(q):
        return lax.rem(offset - (part * batch + q) + side, side)

    @pl.when(active == 1)
    def _():
        @pl.when((gap == 0) & (part == 0))
        def _():
            def clear(n, carry):
                ra[n] = jnp.zeros(ra.shape[1:], F32)
                return carry

            lax.fori_loop(0, ra.shape[0], clear, 0)
            cb[...] = jnp.zeros(cb.shape, F32)

            @pl.when(own == 1)
            def _():
                if EXPLICIT:
                    pltpu.matmul_push_rhs(w[0, 0], 0, 0)
                sweep([(0, 0, 0, base_of(0), w[0, 0])], 0, False, -1)

        def step(n, carry):
            q = 4 * n
            if EXPLICIT:
                for k in range(4):
                    pltpu.matmul_push_rhs(w[0, q + k], k // 2, k % 2)
            for k in (0, 2):
                units = []
                for x in (0, 1):
                    weight = None if EXPLICIT else w[0, q + k + x]
                    units.append((x, k // 2, q + k + x, base_of(q + k + x), weight))
                sweep(units, gap, True, 1)
            return carry

        lax.fori_loop(0, batch // 4, step, 0)

        @pl.when(last)
        def _():
            lane = lax.broadcasted_iota(jnp.int32, (8, 128), 1)

            def row_end(n, carry):
                for g in range(groups):
                    out = jnp.zeros((8, 128), F32)
                    for c in range(half):
                        r = ra[n, c, g]
                        for v in range(half):
                            s = jnp.sum(r * aw[n, v, g], axis=1, keepdims=True)
                            out = jnp.where(lane == half * v + c, s, out)
                    rout[n, g] = out
                return carry

            lax.fori_loop(0, ra.shape[0], row_end, 0)

            def col_end(n, carry):
                for j in range(stride):
                    for g in range(groups):
                        out = jnp.zeros((8, 128), F32)
                        for c in range(half):
                            r = cb[n, j, g, pl.ds(8 * c, 8), :]
                            for v in range(half):
                                s = jnp.sum(r * bw[n, j, g, v], axis=1, keepdims=True)
                                out = jnp.where(lane == half * v + c, s, out)
                        cout[n, j, g] = out
                return carry

            lax.fori_loop(0, lines, col_end, 0)

    @pl.when((active == 0) & last)
    def _():
        rout[...] = jnp.zeros(rout.shape, F32)
        cout[...] = jnp.zeros(cout.shape, F32)


def run_pairs(mesh, scal, screened, mask, au, az, bu, bz, aw, bw, stride, copies, groups):
    lines, side, fourier = screened.shape[0], screened.shape[1], screened.shape[2]
    half = au.shape[1]
    batch = side // 4
    slots, depth = 5, 4
    plan = (lines, stride, groups, side, batch, slots, depth)
    rows = au.shape[0]

    def whole(a):
        zeros = (0,) * a.ndim
        return pl.BlockSpec(a.shape, lambda d, q, s: zeros, pipeline_mode=pl.Buffered(1))

    if True:
        call = pl.pallas_call(
            functools.partial(pair_kernel, plan),
            out_shape=(
                jax.ShapeDtypeStruct((rows, groups, 8, 128), F32),
                jax.ShapeDtypeStruct((lines, stride, groups, 8, 128), F32),
            ),
            grid_spec=pltpu.PrefetchScalarGridSpec(
                num_scalar_prefetch=1,
                grid=(lines, side // batch),
                in_specs=[
                    pl.BlockSpec((1, batch, fourier, fourier), lambda d, q, s: (d * s[1], q * s[1], 0, 0)),
                    pl.BlockSpec(
                        (1, batch, stride, groups, 16, 128), lambda d, q, s: (d * s[1], q * s[1], 0, 0, 0, 0)
                    ),
                ]
                + [whole(a) for a in (au, az, bu, bz, aw, bw)],
                out_specs=(
                    pl.BlockSpec((rows, groups, 8, 128), lambda d, q, s: (0, 0, 0, 0)),
                    pl.BlockSpec((lines, stride, groups, 8, 128), lambda d, q, s: (0, 0, 0, 0, 0)),
                ),
                scratch_shapes=[
                    pltpu.VMEM((rows, half, groups, 8, fourier), F32),
                    pltpu.VMEM((lines, stride, groups, 8 * half, fourier), F32),
                ],
            ),
            compiler_params=pltpu.CompilerParams(
                dimension_semantics=("arbitrary", "arbitrary"), vmem_limit_bytes=60 * 1024 * 1024
            ),
            cost_estimate=pl.CostEstimate(
                flops=2 * lines * side * rows * groups * 8 * half * half * fourier,
                bytes_accessed=screened.size * 2,
                transcendentals=0,
            ),
        )
        return call(scal, screened, mask, au, az, bu, bz, aw, bw)


def spread(arr, axis, copies, shift):
    return jnp.stack([jnp.roll(arr, -e * shift, 0) for e in range(copies)], axis=axis)


def pad_rows(arr, axis, groups):
    extra = groups * 8 - arr.shape[axis]
    if extra:
        widths = [(0, 0)] * arr.ndim
        widths[axis] = (0, extra)
        arr = jnp.pad(arr, widths)
    return arr.reshape(arr.shape[:axis] + (groups, 8) + arr.shape[axis + 1 :])


def contracted(bands, trial):
    half = bands.shape[-2] // 2
    valence = bands[..., half:, :].astype(F32)
    weights = trial.astype(F32).reshape(trial.shape[:-1] + (half, half))
    out = valence[..., 0, None, :] * weights[..., 0, :, None]
    for v in range(1, half):
        out = out + valence[..., v, None, :] * weights[..., v, :, None]
    return out


def panel_tables(bands, trial, stride, copies, groups):
    half = bands.shape[2] // 2

    def table(arr):
        arr = jnp.transpose(arr, (1, 2, 0, 3))
        arr = spread(arr, 2, copies, stride)
        arr = arr.reshape(arr.shape[:2] + (-1, arr.shape[-1]))
        arr = pad_rows(arr, 2, groups)
        return jnp.concatenate([arr, arr[: stride - 1]], axis=0)

    au = table(bands[:, :, :half])
    au = jnp.concatenate([au, au], axis=3)
    return au, table(contracted(bands, trial)), table(bands[:, :, half:].astype(F32))


def column_tables(bands, trial, lines, stride, copies, groups):
    half = bands.shape[2] // 2

    def table(arr):
        out = []
        for gap in range(lines):
            x = arr[gap : gap + lines].reshape((lines, copies, stride) + arr.shape[2:])
            x = jnp.transpose(x, (2, 3, 1, 0, 4))
            x = x.reshape(x.shape[:2] + (-1, x.shape[-1]))
            x = pad_rows(x, 2, groups)
            out.append(jnp.transpose(x, (0, 2, 1, 3, 4)))
        return jnp.stack(out)

    bu = table(bands[:, :, :half])
    bz = table(contracted(bands, trial))
    bw = table(bands[:, :, half:].astype(F32))
    flat = lambda a: a.reshape(a.shape[:3] + (-1, a.shape[-1]))
    return flat(bu), flat(bz), bw


def mask_table(full_mask, first_line, lines, offset, same_line, stride, copies, groups):
    side = full_mask.shape[1]
    padded = jnp.pad(full_mask, ((0, 0), (0, 0), (0, 2 * lines + side)))
    near = lax.dynamic_slice_in_dim(padded, first_line, 2 * lines - 1, 2)
    sel = jnp.stack([jnp.stack([near[t, :, t + gap] for t in range(lines)]) for gap in range(lines)])
    points = jnp.arange(side, dtype=jnp.int32)
    turned = jnp.take(sel, (offset - points) % side, axis=2)
    moved = jnp.stack(
        [
            jnp.stack([jnp.roll(turned, j + stride * e, axis=2) for e in range(copies)])
            for j in range(stride)
        ]
    )
    place = offset + jnp.arange(stride)[:, None] + stride * jnp.arange(copies)[None, :]
    ahead = (points[None, None, :] <= place[:, :, None])[:, :, None, None, :]
    first_gap = (jnp.arange(lines) == 0)[None, None, :, None, None] & same_line
    kept = (moved > 0) & (ahead | ~first_gap)
    kept = jnp.transpose(kept.astype(F32), (2, 4, 0, 1, 3)).reshape(lines, side, stride, copies * lines)
    kept = pad_rows(kept, 3, groups).astype(BF16)
    return jnp.broadcast_to(
        kept[:, :, :, :, None, :, None], kept.shape[:4] + (2, 8, 128)
    ).reshape(kept.shape[:4] + (16, 128))


def local(mesh, band_factors, pair_density, screened, coulomb, window_mask, trial_vector):
    col_count, row_count = lax.axis_size("col"), lax.axis_size("row")
    col_index, row_index = lax.axis_index("col"), lax.axis_index("row")
    mid = col_count // 2
    lines, side, bands, fourier = band_factors.shape
    pairs = pair_density.shape[2]
    half = bands // 2
    row_width = window_mask.shape[1]
    offset = row_index * row_width
    stride, copies, groups = shape_plan(lines, row_width)
    is_lower = col_index < mid

    def gather_rows(part, axis):
        pieces = [part] + [
            lax.ppermute(part, "row", [(i, (i + s) % row_count) for i in range(row_count)])
            for s in range(1, row_count)
        ]
        stacked = jnp.stack(pieces)
        order = (row_index - jnp.arange(row_count)) % row_count
        stacked = jnp.take(stacked, order, axis=0)
        moved = jnp.moveaxis(stacked, 0, axis)
        shape = part.shape[:axis] + (row_count * part.shape[axis],) + part.shape[axis + 1 :]
        return moved.reshape(shape)

    own_bands = lax.dynamic_slice_in_dim(band_factors, offset, row_width, 1)
    own_trial = lax.dynamic_slice_in_dim(trial_vector, offset, row_width, 2)
    own_trial = jnp.transpose(own_trial, (1, 2, 0))
    extra = -(-row_width * pairs // fourier)
    trial_rows = own_trial.reshape(lines, row_width * pairs)
    trial_rows = jnp.pad(trial_rows, ((0, 0), (0, extra * fourier - row_width * pairs)))
    packed = jnp.concatenate(
        [own_bands.reshape(lines, row_width * bands, fourier), trial_rows.reshape(lines, extra, fourier)], axis=1
    )
    first_cols = lax.ppermute(packed, "col", [(i + mid, i) for i in range(mid)])
    next_cols = lax.ppermute(first_cols[: lines - 1], "col", [(i + 1, i) for i in range(mid - 1)])
    panel = first_cols
    reach = mid
    while reach > 1:
        reach //= 2
        sent = lax.ppermute(panel, "col", [(i, i + reach) for i in range(0, mid, 2 * reach)])
        panel = jnp.where((col_index % (2 * reach)) == reach, sent, panel)

    full_mask = gather_rows(window_mask, 1)

    line_first = col_index * lines
    density = pair_density.astype(F32)
    trial = jnp.transpose(trial_vector, (1, 2, 0)).astype(F32)
    scaled = (density * coulomb).astype(BF16).astype(F32)
    dense = jnp.sum(density * trial[..., None], axis=2)
    scaled_sum = jnp.sum(scaled * trial[..., None], axis=2)
    line_sum = jnp.sum(dense, axis=1)
    flat_mask = full_mask.astype(F32)
    reached = jnp.einsum("tba,tbg->ag", flat_mask, scaled_sum, precision=HIGHEST)
    panel_first = lines * mid
    rounds = []
    for s in range(1, mid):
        mine = jnp.where(col_index == mid, reached[panel_first + s * lines : panel_first + (s + 1) * lines], line_sum)
        rounds.append(lax.ppermute(mine, "col", [(mid, mid + s), (mid + s, mid)]))
    all_lines = jnp.concatenate([line_sum] + rounds, axis=0)
    far = rounds[0] if rounds else jnp.zeros_like(line_sum)
    for s in range(2, mid):
        far = jnp.where(col_index == mid + s, rounds[s - 1], far)
    t_index = jnp.arange(lines)
    later = (jnp.arange(lines * mid)[None, :] > t_index[:, None]).astype(F32)
    row_mask = window_mask[:, :, panel_first:].astype(F32)
    q_far = jnp.einsum("tba,ag->tbg", row_mask * later[:, None, :], all_lines, precision=HIGHEST)
    points = jnp.arange(side)
    own_points = offset + jnp.arange(row_width)
    from_on = (points[None, :] >= own_points[:, None]).astype(F32)
    q_own = jnp.einsum("bc,tcg->tbg", from_on, dense, precision=HIGHEST)
    own_gate = jnp.stack([row_mask[t, :, t] for t in range(lines)])
    q_all = q_far + own_gate[..., None] * q_own
    scaled_own = lax.dynamic_slice_in_dim(scaled, offset, row_width, 1)
    row_exchange = 2.0 * jnp.sum(scaled_own * q_all[:, :, None, :], axis=-1)
    row_exchange = jnp.where(col_index == mid, jnp.transpose(row_exchange, (2, 0, 1)), 0.0)
    earlier = (t_index[:, None] > t_index[None, :]).astype(F32)
    near_mask = full_mask[:, :, panel_first : panel_first + lines].astype(F32)
    per_line = jnp.stack([jnp.sum(near_mask[:, :, a, None] * scaled_sum, axis=1) for a in range(lines)])
    v_near = jnp.sum(per_line * earlier[:, :, None], axis=1)
    diag_mask = jnp.stack([near_mask[t, :, t] for t in range(lines)])
    below = (points[None, :] < own_points[:, None]).astype(F32)
    v_own = jnp.einsum("cb,tbg->tcg", below, diag_mask[..., None] * scaled_sum, precision=HIGHEST)
    v_panel = v_near[:, None, :] + v_own
    v_all = jnp.where(col_index == mid, v_panel, far[:, None, :])
    density_own = lax.dynamic_slice_in_dim(density, offset, row_width, 1)
    col_exchange = 2.0 * jnp.sum(density_own * v_all[:, :, None, :], axis=-1)
    col_exchange = jnp.where(is_lower, 0.0, jnp.transpose(col_exchange, (2, 0, 1)))

    panel = gather_rows(panel[:, None], 1)

    def unpack(rows):
        factor = rows[..., : row_width * bands, :]
        factor = factor.reshape(rows.shape[:-2] + (row_width, bands, fourier))
        vector = rows[..., row_width * bands :, :].reshape(rows.shape[:-2] + (-1,))[..., : row_width * pairs]
        return factor, vector.reshape(rows.shape[:-2] + (row_width, pairs))

    panel_bands, panel_trial = unpack(panel)
    panel_bands = panel_bands.reshape(lines, side, bands, fourier)
    panel_trial = panel_trial.reshape(lines, side, pairs)
    col_bands, col_trial = unpack(jnp.concatenate([first_cols, next_cols], axis=0))
    au, az, aw = panel_tables(panel_bands, panel_trial, stride, copies, groups)
    bu, bz, bw = column_tables(col_bands, col_trial, lines, stride, copies, groups)
    kept = mask_table(
        full_mask, panel_first + col_index * lines, lines, offset, col_index == 0, stride, copies, groups
    )
    scal = jnp.stack([offset, is_lower.astype(jnp.int32), (col_index == 0).astype(jnp.int32)])
    rout, cout = run_pairs(mesh, scal, screened, kept, au, az, bu, bz, aw, bw, stride, copies, groups)

    rows = rout.reshape(rout.shape[0], groups * 8, 128)[:, : copies * lines, :pairs]
    rows = rows.reshape(-1, copies, lines, pairs)
    rows = rows[:side] + jnp.pad(rows[side:], ((0, side - stride + 1), (0, 0), (0, 0), (0, 0)))
    row_direct = rows[:, 0]
    for e in range(1, copies):
        row_direct = row_direct + jnp.roll(rows[:, e], stride * e, axis=0)
    row_direct = jnp.transpose(row_direct, (2, 1, 0))
    cols = cout.reshape(lines, stride, groups * 8, 128)[:, :, : copies * lines, :pairs]
    cols = cols.reshape(lines, stride, copies, lines, pairs)
    col_direct = sum(jnp.pad(cols[gap], ((0, 0), (0, 0), (gap, lines - 1 - gap), (0, 0))) for gap in range(lines))
    col_direct = jnp.transpose(col_direct, (3, 2, 1, 0)).reshape(pairs, 2 * lines - 1, row_width)

    back_first = lax.ppermute(col_direct[:, :lines], "col", [(i, i + mid) for i in range(mid)])
    back_next = lax.ppermute(col_direct[:, lines:], "col", [(i, i + mid + 1) for i in range(mid - 1)])
    col_image = col_exchange - back_first - jnp.pad(back_next, ((0, 0), (0, 1), (0, 0)))

    row_part = row_direct.reshape(pairs, lines, row_count, row_width)
    row_part = lax.all_to_all(row_part, "row", 2, 2, tiled=True).sum(axis=2)
    row_part = row_exchange - row_part
    share = pairs // col_count
    row_part = row_part.reshape(col_count, share, lines, row_width)
    row_image = lax.all_to_all(row_part, "col", 0, 0, tiled=True).sum(axis=0)
    return (row_image, col_image)


def solution(mesh):
    placed = (
        P("col", None, None, None),
        P("col", None, None, None),
        P("col", None, None, None),
        P(),
        P(None, "row", None),
        P(None, "col", None),
    )
    return jax.shard_map(
        functools.partial(local, mesh),
        mesh=mesh,
        in_specs=placed,
        out_specs=(P("col", None, "row"), P(None, "col", "row")),
        check_vma=False,
    )
```

```python
import functools
import itertools

import jax
import jax.numpy as jnp
from jax import lax
from jax.experimental import pallas as pl
from jax.experimental.pallas import tpu as pltpu
from jax.sharding import PartitionSpec as P

EXPLICIT = True
SLOTS, DEPTH = 17, 16
HIGHEST = lax.Precision.HIGHEST
F32 = jnp.float32
BF16 = jnp.bfloat16


def shape_plan(lines, row_width):
    best = None
    for copies in range(1, row_width + 1):
        if row_width % copies:
            continue
        used = copies * lines
        groups = -(-used // 8)
        waste = groups * 8 * (row_width // copies)
        if best is None or waste < best[0]:
            best = (waste, copies, groups)
    _, copies, groups = best
    return row_width // copies, copies, groups


def pair_kernel(plan, scal, w, near, after, keep, *refs):
    lines, stride, copies, groups, side, width, bands, batch, slots, depth, pieces = plan
    panel = refs[:pieces]
    rout, cout, factors, columns, au, az, aw, bu, bz, bw, ra, cb = refs[pieces:]
    gap = pl.program_id(0)
    part = pl.program_id(1)
    offset = scal[0]
    active = scal[1]
    own = scal[2]
    half = bands // 2
    last = (gap == pl.num_programs(0) - 1) & (part == pl.num_programs(1) - 1)

    def multiply(chunks, loads, accs):
        if not EXPLICIT:
            for unit, stage, make in chunks:
                yield jnp.dot(make(), loads[unit, stage], preferred_element_type=F32)
            return
        started = [0, 0]
        pending = []
        loaded = set()

        def issue(unit, stage, make):
            slot = accs[unit * slots + started[unit] % slots]
            load = stage if (unit, stage) not in loaded else None
            loaded.add((unit, stage))
            pltpu.matmul_acc_lhs(slot, make(), load_staged_rhs=load)
            started[unit] += 1
            pending.append(slot)

        for chunk in chunks[:depth]:
            issue(*chunk)
        for n in range(len(chunks)):
            if n + depth < len(chunks):
                issue(*chunks[n + depth])
            yield pltpu.matmul_pop(pending.pop(0))

    def sweep(phases, gap_index, with_row, sign, masks):
        chunks = []
        where = []
        for phase in phases:
            for j, g, c in itertools.product(range(stride), range(groups), range(half)):
                    for unit, stage, q, base, _ in phase:

                        def make(j=j, g=g, c=c, q=q, base=base):
                            mk = masks[q][j, g]
                            row = au[base + j, c, g] * jnp.concatenate([mk, mk], axis=1)
                            return jnp.concatenate([row] * (half // 2), axis=0) * bu[gap_index, j, g]

                        chunks.append((unit, stage, make))
                        where.append((j, g, c, base))
        loads = {(unit, stage): weight for phase in phases for unit, stage, _, _, weight in phase}
        if not EXPLICIT:
            consume(multiply(chunks, loads, ()), where, gap_index, with_row, sign)
            return
        spaces = [pltpu.ACC(unit)((8 * half, au.shape[-1]), F32) for unit in (0, 1) for _ in range(slots)]
        pl.run_scoped(
            lambda *accs: consume(multiply(chunks, loads, accs), where, gap_index, with_row, sign), *spaces
        )

    def consume(products, where, gap_index, with_row, sign):
        total = None
        for n, m in enumerate(products):
            j, g, c, base = where[n]
            if with_row:
                p = m * bz[gap_index, j, g]
                s = p[0:8]
                for v in range(1, half):
                    s = s + p[8 * v : 8 * v + 8]
                ra[base + j, c, g] = ra[base + j, c, g] + s
            t = m * jnp.concatenate([az[base + j, c, g]] * half, axis=0)
            total = t if total is None else total + t
            if n + 1 == len(where) or where[n + 1][:2] != (j, g):
                if sign > 0:
                    cb[gap_index, j, g] = cb[gap_index, j, g] + total
                else:
                    cb[gap_index, j, g] = cb[gap_index, j, g] - total
                total = None

    def mask_of(gap_index, base):
        out = {}
        for j, g in itertools.product(range(stride), range(groups)):
            turned = pltpu.roll(keep[gap_index, j, g], 128 - base, 1)
            one = jnp.broadcast_to(turned[:, 0:1], (8, 128))
            out[j, g] = jnp.concatenate([one, one], axis=0).astype(BF16)
        return out

    def grouped(parts):
        extra = groups * 8 - sum(p.shape[0] for p in parts)
        if extra:
            parts = parts + [jnp.zeros((extra, parts[0].shape[1]), F32)]
        merged = jnp.concatenate(parts, axis=0)
        return [merged[8 * g : 8 * g + 8] for g in range(groups)]

    def contract(valence, vector):
        out = []
        for c in range(half):
            z = valence[0] * vector[:, c : c + 1]
            for v in range(1, half):
                z = z + valence[v] * vector[:, half * v + c : half * v + c + 1]
            out.append(z)
        return out

    def build():
        for n in range(pieces):
            place = lax.rem(scal[3] - n + pieces, pieces) * width
            factors[pl.ds(place, width)] = panel[n][...].astype(F32)
        columns[0] = near[...].astype(F32)
        columns[1] = after[...].astype(F32)

        def panel_row(x, carry):
            def rows(band):
                return grouped(
                    [factors[lax.rem(x + stride * e, side), pl.ds(band * lines, lines), :] for e in range(copies)]
                )

            for c in range(half):
                for g, r in enumerate(rows(c)):
                    au[x, c, g] = jnp.concatenate([r, r], axis=0).astype(BF16)
            valence = [rows(half + v) for v in range(half)]
            vector = rows(bands)
            for g in range(groups):
                for v in range(half):
                    aw[x, v, g] = valence[v][g]
                for c, z in enumerate(contract([valence[v][g] for v in range(half)], vector[g])):
                    az[x, c, g] = z
            return carry

        lax.fori_loop(0, side + stride - 1, panel_row, 0)

        def column_row(j, carry):
            for d in range(lines):

                def rows(band):
                    parts = []
                    for e in range(copies):
                        parts.append(columns[0, j + stride * e, pl.ds(band * lines + d, lines - d), :])
                        if d:
                            parts.append(columns[1, j + stride * e, pl.ds(band * lines, d), :])
                    return grouped(parts)

                first = [rows(c) for c in range(half)]
                for g in range(groups):
                    bu[d, j, g] = jnp.concatenate([first[c][g] for c in range(half)], axis=0).astype(BF16)
                valence = [rows(half + v) for v in range(half)]
                vector = rows(bands)
                for g in range(groups):
                    for v in range(half):
                        bw[d, j, g, v] = valence[v][g]
                    z = contract([valence[v][g] for v in range(half)], vector[g])
                    bz[d, j, g] = jnp.concatenate(z, axis=0)
            return carry

        lax.fori_loop(0, stride, column_row, 0)

    def base_of(q):
        return lax.rem(offset - (part * batch + q) + side, side)

    @pl.when(active == 1)
    def _():
        @pl.when((gap == 0) & (part == 0))
        def _():
            build()

            def clear(n, carry):
                ra[n] = jnp.zeros(ra.shape[1:], F32)
                return carry

            lax.fori_loop(0, ra.shape[0], clear, 0)
            cb[...] = jnp.zeros(cb.shape, F32)

            @pl.when(own == 1)
            def _():
                if EXPLICIT:
                    pltpu.matmul_push_rhs(w[0, 0], 0, 0)
                sweep([[(0, 0, 0, base_of(0), w[0, 0])]], 0, False, -1, {0: mask_of(0, base_of(0))})

        def step(n, carry):
            q = 4 * n
            if EXPLICIT:
                for k in range(4):
                    pltpu.matmul_push_rhs(w[0, q + k], k // 2, k % 2)
            phases = []
            masks = {}
            for k in (0, 2):
                units = []
                for x in (0, 1):
                    weight = None if EXPLICIT else w[0, q + k + x]
                    base = base_of(q + k + x)
                    masks[k + x] = mask_of(gap, base)
                    units.append((x, k // 2, k + x, base, weight))
                phases.append(units)
            sweep(phases, gap, True, 1, masks)
            return carry

        lax.fori_loop(0, batch // 4, step, 0)

        @pl.when(last)
        def _():
            lane = lax.broadcasted_iota(jnp.int32, (8, 128), 1)

            def row_end(n, carry):
                for g in range(groups):
                    out = jnp.zeros((8, 128), F32)
                    for c in range(half):
                        r = ra[n, c, g]
                        for v in range(half):
                            s = jnp.sum(r * aw[n, v, g], axis=1, keepdims=True)
                            out = jnp.where(lane == half * v + c, s, out)
                    rout[n, g] = out
                return carry

            lax.fori_loop(0, ra.shape[0], row_end, 0)

            def col_end(n, carry):
                for j in range(stride):
                    for g in range(groups):
                        out = jnp.zeros((8, 128), F32)
                        for c in range(half):
                            r = cb[n, j, g, pl.ds(8 * c, 8), :]
                            for v in range(half):
                                s = jnp.sum(r * bw[n, j, g, v], axis=1, keepdims=True)
                                out = jnp.where(lane == half * v + c, s, out)
                        cout[n, j, g] = out
                return carry

            lax.fori_loop(0, lines, col_end, 0)

    @pl.when((active == 0) & last)
    def _():
        rout[...] = jnp.zeros(rout.shape, F32)
        cout[...] = jnp.zeros(cout.shape, F32)


def run_pairs(scal, screened, near, after, keep, panel, bands, stride, copies, groups):
    lines, side, fourier = screened.shape[0], screened.shape[1], screened.shape[2]
    width = near.shape[0]
    half = bands // 2
    batch = side // 4
    plan = (lines, stride, copies, groups, side, width, bands, batch, SLOTS, DEPTH, len(panel))
    rows = side + stride - 1

    def whole(a):
        zeros = (0,) * a.ndim
        return pl.BlockSpec(a.shape, lambda d, q, s: zeros, pipeline_mode=pl.Buffered(1))

    inputs = (near, after, keep) + tuple(panel)
    call = pl.pallas_call(
        functools.partial(pair_kernel, plan),
        out_shape=(
            jax.ShapeDtypeStruct((rows, groups, 8, 128), F32),
            jax.ShapeDtypeStruct((lines, stride, groups, 8, 128), F32),
        ),
        grid_spec=pltpu.PrefetchScalarGridSpec(
            num_scalar_prefetch=1,
            grid=(lines, side // batch),
            in_specs=[pl.BlockSpec((1, batch, fourier, fourier), lambda d, q, s: (d * s[1], q * s[1], 0, 0))]
            + [whole(a) for a in inputs],
            out_specs=(
                pl.BlockSpec((rows, groups, 8, 128), lambda d, q, s: (0, 0, 0, 0)),
                pl.BlockSpec((lines, stride, groups, 8, 128), lambda d, q, s: (0, 0, 0, 0, 0)),
            ),
            scratch_shapes=[
                pltpu.VMEM((side,) + near.shape[1:], F32),
                pltpu.VMEM((2,) + near.shape, F32),
                pltpu.VMEM((rows, half, groups, 16, fourier), BF16),
                pltpu.VMEM((rows, half, groups, 8, fourier), F32),
                pltpu.VMEM((rows, half, groups, 8, fourier), F32),
                pltpu.VMEM((lines, stride, groups, 8 * half, fourier), BF16),
                pltpu.VMEM((lines, stride, groups, 8 * half, fourier), F32),
                pltpu.VMEM((lines, stride, groups, half, 8, fourier), F32),
                pltpu.VMEM((rows, half, groups, 8, fourier), F32),
                pltpu.VMEM((lines, stride, groups, 8 * half, fourier), F32),
            ],
        ),
        compiler_params=pltpu.CompilerParams(
            dimension_semantics=("arbitrary", "arbitrary"), vmem_limit_bytes=60 * 1024 * 1024
        ),
        cost_estimate=pl.CostEstimate(
            flops=2 * lines * side * rows * groups * 8 * half * half * fourier,
            bytes_accessed=screened.size * 2,
            transcendentals=0,
        ),
    )
    return call(scal, screened, *inputs)


def keep_table(pieces, first_line, row_index, same_line, stride, copies, groups):
    row_count = len(pieces)
    lines, width, side = pieces[0].shape
    stacked = jnp.stack(pieces, axis=1).reshape(lines, row_count * width, side)
    gaps = jnp.arange(lines, dtype=jnp.int32)
    wanted = first_line + gaps[:, None] + gaps[None, :]
    across = jnp.arange(side, dtype=jnp.int32)
    picked = jnp.sum(
        jnp.where(across == wanted[:, :, None, None], stacked[None], 0), axis=3
    )
    order = (row_index - jnp.arange(row_count, dtype=jnp.int32)) % row_count
    held = (order[:, None] * width + jnp.arange(width, dtype=jnp.int32)[None, :]).reshape(-1)
    ahead = jnp.arange(width, dtype=jnp.int32)
    point = (ahead[:, None] + across[None, :]) % side
    chosen = (held[:, None, None] == point[None]).astype(BF16)
    kept = jnp.einsum("gtb,bkm->gktm", picked.astype(BF16), chosen, preferred_element_type=F32)
    later = (point <= row_index * width + ahead[:, None]).astype(F32)
    first_gap = (gaps == 0)[:, None, None, None] & same_line
    kept = kept * jnp.where(first_gap, later[None, :, None, :], 1.0)
    kept = kept.reshape(lines, copies, stride, lines, side)
    kept = jnp.transpose(kept, (0, 2, 1, 3, 4)).reshape(lines, stride, copies * lines, side)
    kept = jnp.pad(kept, ((0, 0), (0, 0), (0, groups * 8 - copies * lines), (0, 128 - side)))
    return kept.reshape(lines, stride, groups, 8, 128)


def local(band_factors, pair_density, screened, coulomb, window_mask, trial_vector):
    col_count, row_count = lax.axis_size("col"), lax.axis_size("row")
    col_index, row_index = lax.axis_index("col"), lax.axis_index("row")
    mid = col_count // 2
    lines, side, bands, fourier = band_factors.shape
    pairs = pair_density.shape[2]
    half = bands // 2
    row_width = window_mask.shape[1]
    offset = row_index * row_width
    stride, copies, groups = shape_plan(lines, row_width)
    is_lower = col_index < mid

    def shared(part):
        return [part] + [
            lax.ppermute(part, "row", [(i, (i + s) % row_count) for i in range(row_count)])
            for s in range(1, row_count)
        ]

    mask_pieces = shared(window_mask)
    own_bands = lax.dynamic_slice_in_dim(band_factors, offset, row_width, 1)
    own_trial = jnp.transpose(lax.dynamic_slice_in_dim(trial_vector, offset, row_width, 2), (1, 2, 0))
    own_trial = jnp.pad(own_trial, ((0, 0), (0, 0), (0, fourier - pairs)))
    packed = jnp.concatenate([own_bands, own_trial[:, :, None, :]], axis=2)
    packed = jnp.transpose(packed, (1, 2, 0, 3)).reshape(row_width, (bands + 1) * lines, fourier)
    near = lax.ppermute(packed, "col", [(i + mid, i) for i in range(mid)])
    panel = near
    reach = mid
    while reach > 1:
        reach //= 2
        sent = lax.ppermute(panel, "col", [(i, i + reach) for i in range(0, mid, 2 * reach)])
        panel = jnp.where((col_index % (2 * reach)) == reach, sent, panel)
    panel_pieces = [panel] + [
        lax.ppermute(
            panel,
            ("row", "col"),
            [(r * col_count + i, (r + s) % row_count * col_count + i) for r in range(row_count) for i in range(mid)],
        )
        for s in range(1, row_count)
    ]
    after = lax.ppermute(near, "col", [(i + 1, i) for i in range(mid - 1)])
    panel_first = lines * mid
    keep = keep_table(
        mask_pieces, panel_first + col_index * lines, row_index, col_index == 0, stride, copies, groups
    )
    scal = jnp.stack([offset, is_lower.astype(jnp.int32), (col_index == 0).astype(jnp.int32), row_index])

    trial = jnp.transpose(trial_vector, (1, 2, 0)).astype(F32)
    points = jnp.arange(side)
    own_points = offset + jnp.arange(row_width)
    t_index = jnp.arange(lines)
    order = (row_index - jnp.arange(row_count)) % row_count

    def whole_mask():
        full = jnp.take(jnp.stack(mask_pieces), order, axis=0)
        return jnp.transpose(full, (1, 0, 2, 3)).reshape(lines, side, side).astype(F32)

    def first_stage():
        density = pair_density.astype(F32)
        scaled = (density * coulomb).astype(BF16).astype(F32)
        dense = jnp.sum(density * trial[..., None], axis=2)
        scaled_sum = jnp.sum(scaled * trial[..., None], axis=2)
        line_sum = jnp.sum(dense, axis=1)
        reached = jnp.einsum("tba,tbg->ag", whole_mask(), scaled_sum, precision=HIGHEST)
        return dense, scaled_sum, line_sum, reached

    shapes = jax.eval_shape(first_stage)
    nothing = lambda shapes: jax.tree.map(lambda a: jnp.zeros(a.shape, a.dtype), shapes)
    dense, scaled_sum, line_sum, reached = lax.cond(is_lower, lambda: nothing(shapes), first_stage)
    rounds = []
    for s in range(1, mid):
        mine = jnp.where(col_index == mid, reached[panel_first + s * lines : panel_first + (s + 1) * lines], line_sum)
        rounds.append(lax.ppermute(mine, "col", [(mid, mid + s), (mid + s, mid)]))

    rout, cout = run_pairs(scal, screened, near, after, keep, panel_pieces, bands, stride, copies, groups)

    def second_stage(rounds):
        full_mask = whole_mask()
        density_own = lax.dynamic_slice_in_dim(pair_density, offset, row_width, 1).astype(F32)
        scaled_own = (density_own * coulomb).astype(BF16).astype(F32)
        all_lines = jnp.concatenate([line_sum] + rounds, axis=0)
        far = rounds[0]
        for s in range(2, mid):
            far = jnp.where(col_index == mid + s, rounds[s - 1], far)
        later = (jnp.arange(lines * mid)[None, :] > t_index[:, None]).astype(F32)
        row_mask = window_mask[:, :, panel_first:].astype(F32)
        q_far = jnp.einsum("tba,ag->tbg", row_mask * later[:, None, :], all_lines, precision=HIGHEST)
        from_on = (points[None, :] >= own_points[:, None]).astype(F32)
        q_own = jnp.einsum("bc,tcg->tbg", from_on, dense, precision=HIGHEST)
        own_gate = jnp.stack([row_mask[t, :, t] for t in range(lines)])
        q_all = q_far + own_gate[..., None] * q_own
        row_exchange = 2.0 * jnp.sum(scaled_own * q_all[:, :, None, :], axis=-1)
        row_exchange = jnp.where(col_index == mid, jnp.transpose(row_exchange, (2, 0, 1)), 0.0)
        earlier = (t_index[:, None] > t_index[None, :]).astype(F32)
        near_mask = full_mask[:, :, panel_first : panel_first + lines]
        per_line = jnp.einsum("tba,tbg->atg", near_mask, scaled_sum, precision=HIGHEST)
        v_near = jnp.sum(per_line * earlier[:, :, None], axis=1)
        diag_mask = jnp.stack([near_mask[t, :, t] for t in range(lines)])
        below = (points[None, :] < own_points[:, None]).astype(F32)
        v_own = jnp.einsum("cb,tbg->tcg", below, diag_mask[..., None] * scaled_sum, precision=HIGHEST)
        v_panel = v_near[:, None, :] + v_own
        v_all = jnp.where(col_index == mid, v_panel, far[:, None, :])
        col_exchange = 2.0 * jnp.sum(density_own * v_all[:, :, None, :], axis=-1)
        return row_exchange, jnp.transpose(col_exchange, (2, 0, 1))

    shapes = jax.eval_shape(second_stage, rounds)
    rout, rounds = lax.optimization_barrier((rout, rounds))
    row_exchange, col_exchange = lax.cond(is_lower, lambda _: nothing(shapes), second_stage, rounds)

    rows = rout.reshape(rout.shape[0], groups * 8, 128)[:, : copies * lines, :pairs]
    rows = rows.reshape(-1, copies, lines, pairs)
    rows = rows[:side] + jnp.pad(rows[side:], ((0, side - stride + 1), (0, 0), (0, 0), (0, 0)))
    row_direct = rows[:, 0]
    for e in range(1, copies):
        row_direct = row_direct + jnp.roll(rows[:, e], stride * e, axis=0)
    row_direct = jnp.transpose(row_direct, (2, 1, 0))
    cols = cout.reshape(lines, stride, groups * 8, 128)[:, :, : copies * lines, :pairs]
    cols = cols.reshape(lines, stride, copies, lines, pairs)
    col_direct = sum(jnp.pad(cols[gap], ((0, 0), (0, 0), (gap, lines - 1 - gap), (0, 0))) for gap in range(lines))
    col_direct = jnp.transpose(col_direct, (3, 2, 1, 0)).reshape(pairs, 2 * lines - 1, row_width)

    back_first = lax.ppermute(col_direct[:, :lines], "col", [(i, i + mid) for i in range(mid)])
    back_next = lax.ppermute(col_direct[:, lines:], "col", [(i, i + mid + 1) for i in range(mid - 1)])
    col_image = col_exchange - back_first - jnp.pad(back_next, ((0, 0), (0, 1), (0, 0)))

    row_part = row_direct.reshape(pairs, lines, row_count, row_width)
    row_part = lax.all_to_all(row_part, "row", 2, 2, tiled=True).sum(axis=2)
    row_part = row_exchange - row_part
    share = pairs // col_count
    row_part = row_part.reshape(col_count, share, lines, row_width)
    row_image = lax.all_to_all(row_part, "col", 0, 0, tiled=True).sum(axis=0)
    return (row_image, col_image)


def solution(mesh):
    placed = (
        P("col", None, None, None),
        P("col", None, None, None),
        P("col", None, None, None),
        P(),
        P(None, "row", None),
        P(None, "col", None),
    )
    return jax.shard_map(
        local,
        mesh=mesh,
        in_specs=placed,
        out_specs=(P("col", None, "row"), P(None, "col", "row")),
        check_vma=False,
    )
```
